256 devices in a mesh: row: 32 (over z, x), src: 8 (over y, core).
Axes of the slice: x: 4, y: 4, z: 8, core: 2. Of those that a mesh axis runs over, the one named last changes fastest.
Arguments:
- sub_source: float32 [32768, 4096], P('row', 'src'), may hold values from -6 to 6
- sub_inverse: bfloat16 [32768, 1024], P('row'), as said below
- coupling: bfloat16 [32, 2, 512, 1024], P('row'), may hold values from -0.0625 to 0.0625
- update_lists: int32 [32, 2], P('row'), may hold values from 0 to 3, as said below
- sep_source: float32 [2048, 4096], P('row', 'src'), may hold values from -6 to 6
- sep_inverse: bfloat16 [16384, 512], P(('row', 'src')), as said below
- sep_lower: bfloat16 [16384, 1024], P(('row', 'src')), may hold values from -0.125 to 0.125
- factor_owner_slots: int32 [4], replicated, may hold values from 0 to 31, as said below
- sep_links: int32 [4, 2], replicated, may hold values from -1 to 2, as said below
Outputs:
- sub_field: float32 [32768, 4096], P('row', 'src')
- sep_field: float32 [2048, 4096], P('row', 'src')
The draws below stay inside these ranges and needn't reach their ends.
Inputs may be any that keep to these rules, and one draw needn't show every extreme that they name: `update_lists`: each subtree lists two different separator blocks. `factor_owner_slots`: the 4 entries are different slots. `sep_links`: for block k the first entry is k - 1 and the second is -1 or a block below k - 1; -1 means no link. `sub_inverse`: each slot of 1024 rows is lower triangular. `sep_inverse`: each slot of 512 rows is lower triangular.
All inputs are finite; a program needn't handle non-finite values.
Results may differ from the reference program's by a relative error of at most 0.006.
Values may be sent and summed in bfloat16 or wider, within the bound.
A program may use at most 64 MiB of HBM per device.

```python
import math
import jax
import jax.numpy as jnp
from jax import lax

SUB_ROWS = 1024
SEP_BLOCK = 512
STEPS = 4
LISTED = 2
LINKS = 2
SEP_ROWS = 2048
SOURCES = 4096
N_ROW = 32


def triangle(rough, diagonal, slots, order):
    rows = lax.broadcasted_iota(jnp.int32, (slots, order, order), 1)
    cols = lax.broadcasted_iota(jnp.int32, (slots, order, order), 2)
    strictly_lower = rough * (1.0 / math.sqrt(order))
    return jnp.where(rows > cols, strictly_lower, jnp.where(rows == cols, diagonal, 0.0))


def draw_sub_inverse(key, part):
    first, second = jax.random.split(jax.random.fold_in(key, 5))
    shape = (N_ROW, SUB_ROWS, SUB_ROWS)
    rough = jax.random.normal(first, shape, jnp.float32)
    diagonal = jax.random.uniform(second, shape, jnp.float32, 0.8, 1.6)
    full = triangle(rough, diagonal, N_ROW, SUB_ROWS)
    return full.reshape(N_ROW * SUB_ROWS, SUB_ROWS).astype(jnp.bfloat16)


def draw_sep_inverse(key, part):
    first, second = jax.random.split(jax.random.fold_in(key, 7))
    shape = (N_ROW, SEP_BLOCK, SEP_BLOCK)
    rough = jax.random.normal(first, shape, jnp.float32)
    diagonal = jax.random.uniform(second, shape, jnp.float32, 0.8, 1.6)
    full = triangle(rough, diagonal, N_ROW, SEP_BLOCK)
    return full.reshape(N_ROW * SEP_BLOCK, SEP_BLOCK).astype(jnp.bfloat16)


def draw_factor_owner_slots(key, part):
    first, second = jax.random.split(jax.random.fold_in(key, 11))
    middle = 1 + jax.random.permutation(first, N_ROW - 2)[:STEPS - 2]
    values = jnp.concatenate([jnp.array([0, N_ROW - 1], jnp.int32), middle.astype(jnp.int32)])
    return jax.random.permutation(second, values).astype(jnp.int32)


def draw_update_lists(key, part):
    first_key, step_key, forced_key = jax.random.split(jax.random.fold_in(key, 23), 3)
    first = jax.random.randint(first_key, (N_ROW,), 0, STEPS, jnp.int32)
    offset = jax.random.randint(step_key, (N_ROW,), 1, STEPS, jnp.int32)
    forced = jax.random.randint(forced_key, (), 0, N_ROW, jnp.int32)
    device_ids = jnp.arange(N_ROW, dtype=jnp.int32)
    first = jnp.where(device_ids == forced, 0, first)
    offset = jnp.where(device_ids == forced, STEPS - 1, offset)
    second = (first + offset) % STEPS
    return jnp.stack([first, second], axis=1).astype(jnp.int32)


def draw_sep_links(key, part):
    block_ids = jnp.arange(STEPS, dtype=jnp.int32)
    first = block_ids - 1
    drawn = jax.random.randint(jax.random.fold_in(key, 37), (STEPS,), 0, 1 << 20, jnp.int32)
    second = drawn % jnp.maximum(block_ids, 1) - 1
    return jnp.stack([first, second], axis=1).astype(jnp.int32)


def block_scale(stream_key, extent, cuts, least, high):
    def one(axis_at, parts):
        steps = jax.random.uniform(jax.random.fold_in(jax.random.fold_in(stream_key, 6), axis_at), (parts,), jnp.float32, least / len(cuts), high / len(cuts))
        return jnp.repeat(jnp.exp(steps), extent[axis_at] // parts).reshape((-1,) + (1,) * (len(extent) - axis_at - 1))

    gain = one(*cuts[0])
    for cut in cuts[1:]:
        gain = gain * one(*cut)
    return gain


def gaussian(own_key, extent, deviation, limit, shards=(), held_as=jnp.bfloat16):
    values = deviation * jax.random.normal(own_key, extent, jnp.float32)
    if shards:
        values = values * block_scale(own_key, extent, shards, -0.22, 0.18)
    return jnp.clip(values, -limit, limit).astype(held_as)


def setup_inputs(seed: int = 0) -> dict:
    keys = jax.random.split(jax.random.key(seed), 10)
    sub_source = gaussian(keys[0], (N_ROW * SUB_ROWS, SOURCES), 1.0, 6.0, ((0, 32), (1, 8)), jnp.float32)
    sub_inverse = draw_sub_inverse(jax.random.fold_in(keys[9], 71), 0)
    coupling = gaussian(keys[2], (N_ROW, LISTED, SEP_BLOCK, SUB_ROWS), (8 * SUB_ROWS) ** -0.5, 0.0625, ((0, 32),))
    update_lists = draw_update_lists(jax.random.fold_in(keys[9], 71), 0)
    sep_source = gaussian(keys[4], (SEP_ROWS, SOURCES), 1.0, 6.0, ((0, 32), (1, 8)), jnp.float32)
    sep_inverse = draw_sep_inverse(jax.random.fold_in(keys[9], 71), 0)
    sep_lower = gaussian(keys[6], (N_ROW * SEP_BLOCK, LINKS * SEP_BLOCK), (4 * SEP_BLOCK) ** -0.5, 0.125, ((0, 256),))
    factor_owner_slots = draw_factor_owner_slots(jax.random.fold_in(keys[9], 71), 0)
    sep_links = draw_sep_links(jax.random.fold_in(keys[9], 71), 0)
    return dict(sub_source=sub_source, sub_inverse=sub_inverse, coupling=coupling, update_lists=update_lists, sep_source=sep_source, sep_inverse=sep_inverse, sep_lower=sep_lower, factor_owner_slots=factor_owner_slots, sep_links=sep_links)


def solve_one(operands):
    return jnp.dot(operands[0], operands[1].astype(jnp.bfloat16), preferred_element_type=jnp.float32)


def reference(sub_source, sub_inverse, coupling, update_lists, sep_source, sep_inverse, sep_lower, factor_owner_slots, sep_links):
    sources = sub_source.shape[1]
    inverse_stack = sub_inverse.reshape(N_ROW, SUB_ROWS, SUB_ROWS)
    source_stack = sub_source.reshape(N_ROW, SUB_ROWS, sources)
    sub_field = lax.map(solve_one, (inverse_stack, source_stack))
    padded_length = sub_field.astype(jnp.bfloat16)
    pending = sep_source.reshape(STEPS, SEP_BLOCK, sources)
    for device in range(N_ROW):
        for listed in range(LISTED):
            update = jnp.dot(coupling[device, listed], padded_length[device], preferred_element_type=jnp.float32)
            pending = pending.at[update_lists[device, listed]].add(-update)
    inverse_slots = sep_inverse.reshape(N_ROW, SEP_BLOCK, SEP_BLOCK)
    lower_slots = sep_lower.reshape(N_ROW, SEP_BLOCK, LINKS * SEP_BLOCK)
    solved = jnp.zeros((STEPS, SEP_BLOCK, sources), jnp.float32)
    for block_id in range(STEPS):
        owner_row = factor_owner_slots[block_id]
        pieces = []
        for link_pos in range(LINKS):
            target = sep_links[block_id, link_pos]
            chosen = solved[jnp.maximum(target, 0)]
            pieces.append(jnp.where(target >= 0, chosen, 0.0).astype(jnp.bfloat16))
        stacked = jnp.concatenate(pieces, axis=0)
        remaining_source = pending[block_id] - jnp.dot(lower_slots[owner_row], stacked, preferred_element_type=jnp.float32)
        result = jnp.dot(inverse_slots[owner_row], remaining_source.astype(jnp.bfloat16), preferred_element_type=jnp.float32)
        solved = solved.at[block_id].set(result)
    return sub_field.reshape(N_ROW * SUB_ROWS, sources), solved.reshape(SEP_ROWS, sources)
```

```python
import jax
import jax.numpy as jnp
from jax import lax
from jax.sharding import PartitionSpec as P

STEPS = 4
LINKS = 2
PAIR = 2


def gather_row(x, n_row):
    spread = jnp.broadcast_to(x[None], (n_row,) + x.shape)
    return lax.all_to_all(spread, "row", 0, 0, tiled=False)


def per_device(
    sub_source,
    sub_inverse,
    coupling,
    update_lists,
    sep_source,
    sep_inverse,
    sep_lower,
    factor_owner_slots,
    sep_links,
):
    n_row = lax.psum(1, "row")
    n_src = lax.psum(1, "src")
    cols = sub_source.shape[1]
    local_rows = sep_source.shape[0]
    block = sep_inverse.shape[1]
    span = PAIR * n_src
    my_row = lax.axis_index("row")

    sub_field = jnp.dot(
        sub_inverse, sub_source.astype(jnp.bfloat16), preferred_element_type=jnp.float32
    )
    rounded = sub_field.astype(jnp.bfloat16)
    updates = jnp.einsum(
        "lmf,ft->lmt", coupling[0], rounded, preferred_element_type=jnp.float32
    )
    per_dest = updates.reshape(LINKS, n_src, n_row, PAIR, cols).transpose(2, 0, 1, 3, 4)
    per_dest = per_dest.reshape(n_row, LINKS * span, cols)
    src_rows = sep_source.reshape(n_row, PAIR, cols)
    lists = jnp.zeros((cols,), jnp.float32).at[:LINKS].set(update_lists[0].astype(jnp.float32))
    lists = jnp.broadcast_to(lists[None, None], (n_row, 1, cols))
    payload = jnp.concatenate([per_dest, src_rows, lists], axis=1)
    got = lax.all_to_all(payload, "row", 0, 0, tiled=False)
    got_updates = got[:, : LINKS * span].reshape(n_row, LINKS, span, cols)
    got_src = got[:, LINKS * span : LINKS * span + PAIR].reshape(STEPS, span, cols)
    got_lists = got[:, LINKS * span + PAIR, :LINKS]
    pending = []
    for k in range(STEPS):
        hit = (got_lists == k)[:, :, None, None]
        pending.append(got_src[k] - jnp.sum(jnp.where(hit, got_updates, 0.0), axis=(0, 1)))

    factors = jnp.concatenate([sep_lower, sep_inverse], axis=1)
    width = factors.shape[1]
    slot_rows = lax.all_to_all(factors.reshape(n_row, PAIR, width), "row", 0, 0, tiled=False)
    owned = slot_rows[factor_owner_slots]
    owned = lax.all_gather(owned, "src", axis=0, tiled=False)
    owned = owned.transpose(1, 0, 2, 3).reshape(STEPS, span, width)
    lower_rows = owned[:, :, : LINKS * block]
    inverse_rows = owned[:, :, LINKS * block :]
    inverse_all = lax.all_gather(inverse_rows, "row", axis=0, tiled=False)
    inverse_full = inverse_all.reshape(n_row, STEPS, n_src, PAIR, block)
    inverse_full = inverse_full.transpose(1, 2, 0, 3, 4).reshape(STEPS, block, block)

    solved = jnp.zeros((STEPS, block, cols), jnp.float32)
    for k in range(STEPS):
        pieces = []
        for link_pos in range(LINKS):
            target = sep_links[k, link_pos]
            chosen = solved[jnp.maximum(target, 0)]
            pieces.append(jnp.where(target >= 0, chosen, 0.0).astype(jnp.bfloat16))
        stacked = jnp.concatenate(pieces, axis=0)
        residue = pending[k] - jnp.dot(
            lower_rows[k], stacked, preferred_element_type=jnp.float32
        )
        everyone = gather_row(residue.astype(jnp.bfloat16), n_row)
        everyone = everyone.reshape(n_row, n_src, PAIR, cols).transpose(1, 0, 2, 3)
        full_residue = everyone.reshape(block, cols)
        result = jnp.dot(inverse_full[k], full_residue, preferred_element_type=jnp.float32)
        solved = solved.at[k].set(result)
    whole_field = solved.reshape(STEPS * block, cols)
    own_rows = lax.dynamic_slice_in_dim(whole_field, my_row * local_rows, local_rows, 0)
    return (sub_field, own_rows)


def solution(mesh):
    return jax.shard_map(
        per_device,
        mesh=mesh,
        in_specs=(
            P("row", "src"),
            P("row", None),
            P("row", None, None, None),
            P("row", None),
            P("row", "src"),
            P(("row", "src"), None),
            P(("row", "src"), None),
            P(),
            P(),
        ),
        out_specs=(P("row", "src"), P("row", "src")),
        check_vma=False,
    )
```

```python
import jax
import jax.numpy as jnp
from jax import lax
from jax.sharding import PartitionSpec as P

STEPS = 4
LINKS = 2
PAIR = 2


def gather_row(x, n_row):
    spread = jnp.broadcast_to(x[None], (n_row,) + x.shape)
    return lax.all_to_all(spread, "row", 0, 0, tiled=False)


def per_device(
    sub_source,
    sub_inverse,
    coupling,
    update_lists,
    sep_source,
    sep_inverse,
    sep_lower,
    factor_owner_slots,
    sep_links,
):
    n_row = lax.psum(1, "row")
    n_src = lax.psum(1, "src")
    cols = sub_source.shape[1]
    local_rows = sep_source.shape[0]
    block = sep_inverse.shape[1]
    span = PAIR * n_src
    my_row = lax.axis_index("row")

    factors = jnp.concatenate([sep_lower, sep_inverse], axis=1)
    width = factors.shape[1]
    slot_rows = lax.all_to_all(factors.reshape(n_row, PAIR, width), "row", 0, 0, tiled=False)
    owned = slot_rows[factor_owner_slots]
    owned = owned.reshape(STEPS, PAIR, width // block, n_src, n_row, PAIR)
    owned = owned.transpose(0, 1, 2, 4, 3, 5).reshape(STEPS, PAIR, width)
    owned = lax.all_gather(owned, "src", axis=0, tiled=False)
    owned, sub_source = lax.optimization_barrier((owned, sub_source))
    owned = owned.transpose(1, 0, 2, 3).reshape(STEPS, span, width)
    lower_rows = owned[:, :, : LINKS * block]
    inverse_rows = owned[:, :, LINKS * block :]
    inverse_all = lax.all_gather(inverse_rows, "row", axis=0, tiled=False)

    sub_field = jnp.dot(
        sub_inverse, sub_source.astype(jnp.bfloat16), preferred_element_type=jnp.float32
    )
    rounded = sub_field.astype(jnp.bfloat16)
    updates = jnp.einsum(
        "lmf,ft->lmt", coupling[0], rounded, preferred_element_type=jnp.float32
    )
    per_dest = updates.astype(jnp.bfloat16).reshape(LINKS, n_src, n_row, PAIR, cols)
    per_dest = per_dest.transpose(2, 0, 1, 3, 4).reshape(n_row, LINKS * span, cols)
    src_rows = sep_source.astype(jnp.bfloat16).reshape(n_row, PAIR, cols)
    lists = jnp.zeros((cols,), jnp.bfloat16).at[:LINKS].set(update_lists[0].astype(jnp.bfloat16))
    lists = jnp.broadcast_to(lists[None, None], (n_row, 1, cols))
    payload = jnp.concatenate([per_dest, src_rows, lists], axis=1)
    got = lax.all_to_all(payload, "row", 0, 0, tiled=False).astype(jnp.float32)
    got_updates = got[:, : LINKS * span].reshape(n_row, LINKS, span, cols)
    got_src = got[:, LINKS * span : LINKS * span + PAIR].reshape(STEPS, span, cols)
    got_lists = got[:, LINKS * span + PAIR, :LINKS]
    pending = []
    for k in range(STEPS):
        hit = (got_lists == k)[:, :, None, None]
        pending.append(got_src[k] - jnp.sum(jnp.where(hit, got_updates, 0.0), axis=(0, 1)))

    solved = jnp.zeros((STEPS, block, cols), jnp.float32)
    for k in range(STEPS):
        pieces = []
        for link_pos in range(LINKS):
            target = sep_links[k, link_pos]
            chosen = solved[jnp.maximum(target, 0)]
            pieces.append(jnp.where(target >= 0, chosen, 0.0).astype(jnp.bfloat16))
        stacked = jnp.concatenate(pieces, axis=0)
        residue = pending[k] - jnp.dot(
            lower_rows[k], stacked, preferred_element_type=jnp.float32
        )
        everyone = gather_row(residue.astype(jnp.bfloat16), n_row)
        full_residue = everyone.reshape(block, cols)
        inverse = inverse_all[:, k].reshape(block, block)
        result = jnp.dot(inverse, full_residue, preferred_element_type=jnp.float32)
        solved = solved.at[k].set(result)
    blocks_per = block // local_rows
    whole_field = solved.reshape(STEPS, n_row, n_src, PAIR, cols)
    own_rows = lax.dynamic_slice(
        whole_field,
        (my_row // blocks_per, 0, my_row % blocks_per, 0, 0),
        (1, n_row, 1, PAIR, cols),
    ).reshape(local_rows, cols)
    return (sub_field, own_rows)


def solution(mesh):
    return jax.shard_map(
        per_device,
        mesh=mesh,
        in_specs=(
            P("row", "src"),
            P("row", None),
            P("row", None, None, None),
            P("row", None),
            P("row", "src"),
            P(("row", "src"), None),
            P(("row", "src"), None),
            P(),
            P(),
        ),
        out_specs=(P("row", "src"), P("row", "src")),
        check_vma=False,
    )
```

```python
import jax
import jax.numpy as jnp
from jax import lax
from jax.sharding import PartitionSpec as P

STEPS = 4
LINKS = 2
PAIR = 2


def gather_row(x, n_row):
    spread = jnp.broadcast_to(x[None], (n_row,) + x.shape)
    return lax.all_to_all(spread, "row", 0, 0, tiled=False)


def per_device(
    sub_source,
    sub_inverse,
    coupling,
    update_lists,
    sep_source,
    sep_inverse,
    sep_lower,
    factor_owner_slots,
    sep_links,
):
    n_row = lax.psum(1, "row")
    n_src = lax.psum(1, "src")
    cols = sub_source.shape[1]
    local_rows = sep_source.shape[0]
    block = sep_inverse.shape[1]
    span = PAIR * n_src
    my_row = lax.axis_index("row")

    sub_field = jnp.dot(
        sub_inverse, sub_source.astype(jnp.bfloat16), preferred_element_type=jnp.float32
    )
    rounded = sub_field.astype(jnp.bfloat16)
    updates = jnp.einsum(
        "lmf,ft->lmt", coupling[0], rounded, preferred_element_type=jnp.float32
    )
    per_dest = updates.reshape(LINKS, n_src, n_row, PAIR, cols).transpose(2, 0, 1, 3, 4)
    per_dest = per_dest.reshape(n_row, LINKS * span, cols)
    src_rows = sep_source.reshape(n_row, PAIR, cols)
    lists = jnp.zeros((cols,), jnp.float32).at[:LINKS].set(update_lists[0].astype(jnp.float32))
    lists = jnp.broadcast_to(lists[None, None], (n_row, 1, cols))
    payload = jnp.concatenate([per_dest, src_rows, lists], axis=1)
    got = lax.all_to_all(payload, "row", 0, 0, tiled=False)
    got_updates = got[:, : LINKS * span].reshape(n_row, LINKS, span, cols)
    got_src = got[:, LINKS * span : LINKS * span + PAIR].reshape(STEPS, span, cols)
    got_lists = got[:, LINKS * span + PAIR, :LINKS]
    pending = []
    for k in range(STEPS):
        hit = (got_lists == k)[:, :, None, None]
        pending.append(got_src[k] - jnp.sum(jnp.where(hit, got_updates, 0.0), axis=(0, 1)))

    factors = jnp.concatenate([sep_lower, sep_inverse], axis=1)
    width = factors.shape[1]
    slot_rows = lax.all_to_all(factors.reshape(n_row, PAIR, width), "row", 0, 0, tiled=False)
    owned = slot_rows[factor_owner_slots]
    owned = lax.all_gather(owned, "src", axis=0, tiled=False)
    owned = owned.transpose(1, 0, 2, 3).reshape(STEPS, span, width)
    lower_rows = owned[:, :, : LINKS * block]
    inverse_rows = owned[:, :, LINKS * block :]
    seg = block // n_src
    inverse_rows = inverse_rows.reshape(STEPS, n_src, PAIR, block)
    packed = jnp.concatenate(
        [inverse_rows[:, s, :, : (s + 1) * seg].reshape(STEPS, -1) for s in range(n_src)], axis=1
    )
    packed = lax.all_gather(packed, "row", axis=0, tiled=False)
    pieces, at = [], 0
    for s in range(n_src):
        size = PAIR * (s + 1) * seg
        piece = packed[:, :, at : at + size].reshape(n_row, STEPS, PAIR, (s + 1) * seg)
        pieces.append(jnp.pad(piece, ((0, 0), (0, 0), (0, 0), (0, block - (s + 1) * seg))))
        at += size
    inverse_full = jnp.stack(pieces, axis=0)
    inverse_full = inverse_full.transpose(2, 0, 1, 3, 4).reshape(STEPS, block, block)

    solved = jnp.zeros((STEPS, block, cols), jnp.float32)
    for k in range(STEPS):
        pieces = []
        for link_pos in range(LINKS):
            target = sep_links[k, link_pos]
            chosen = solved[jnp.maximum(target, 0)]
            pieces.append(jnp.where(target >= 0, chosen, 0.0).astype(jnp.bfloat16))
        stacked = jnp.concatenate(pieces, axis=0)
        residue = pending[k] - jnp.dot(
            lower_rows[k], stacked, preferred_element_type=jnp.float32
        )
        everyone = gather_row(residue.astype(jnp.bfloat16), n_row)
        everyone = everyone.reshape(n_row, n_src, PAIR, cols).transpose(1, 0, 2, 3)
        full_residue = everyone.reshape(block, cols)
        result = jnp.dot(inverse_full[k], full_residue, preferred_element_type=jnp.float32)
        solved = solved.at[k].set(result)
    whole_field = solved.reshape(STEPS * block, cols)
    own_rows = lax.dynamic_slice_in_dim(whole_field, my_row * local_rows, local_rows, 0)
    return (sub_field, own_rows)


def solution(mesh):
    return jax.shard_map(
        per_device,
        mesh=mesh,
        in_specs=(
            P("row", "src"),
            P("row", None),
            P("row", None, None, None),
            P("row", None),
            P("row", "src"),
            P(("row", "src"), None),
            P(("row", "src"), None),
            P(),
            P(),
        ),
        out_specs=(P("row", "src"), P("row", "src")),
        check_vma=False,
    )
```

```python
import jax
import jax.numpy as jnp
from jax import lax
from jax.sharding import PartitionSpec as P

STEPS = 4
LINKS = 2
PAIR = 2


def gather_row(x, n_row):
    spread = jnp.broadcast_to(x[None], (n_row,) + x.shape)
    return lax.all_to_all(spread, "row", 0, 0, tiled=False)


def solve(
    sub_source,
    sub_inverse,
    coupling,
    update_lists,
    sep_source,
    sep_inverse,
    sep_lower,
    factor_owner_slots,
    sep_links,
):
    n_row = lax.psum(1, "row")
    n_src = lax.psum(1, "src")
    cols = sub_source.shape[1]
    local_rows = sep_source.shape[0]
    block = sep_inverse.shape[1]
    span = PAIR * n_src
    my_row = lax.axis_index("row")

    factors = jnp.concatenate([sep_lower, sep_inverse], axis=1)
    width = factors.shape[1]
    slot_rows = lax.all_to_all(factors.reshape(n_row, PAIR, width), "row", 0, 0, tiled=False)
    owned = slot_rows[factor_owner_slots]
    owned = owned.reshape(STEPS, PAIR, width // block, n_src, n_row, PAIR)
    owned = owned.transpose(0, 1, 2, 4, 3, 5).reshape(STEPS, PAIR, width)
    owned = lax.all_gather(owned, "src", axis=0, tiled=False)

    sub_field = jnp.dot(
        sub_inverse, sub_source.astype(jnp.bfloat16), preferred_element_type=jnp.float32
    )
    rounded = sub_field.astype(jnp.bfloat16)
    updates = jnp.einsum(
        "lmf,ft->lmt", coupling[0], rounded, preferred_element_type=jnp.float32
    )
    per_dest = updates.reshape(LINKS, n_src, n_row, PAIR, cols).transpose(2, 0, 1, 3, 4)
    per_dest = per_dest.reshape(n_row, LINKS * span, cols)
    src_rows = sep_source.reshape(n_row, PAIR, cols)
    lists = jnp.zeros((cols,), jnp.float32).at[:LINKS].set(update_lists[0].astype(jnp.float32))
    lists = jnp.broadcast_to(lists[None, None], (n_row, 1, cols))
    payload = jnp.concatenate([per_dest, src_rows, lists], axis=1)
    owned = owned.transpose(1, 0, 2, 3).reshape(STEPS, span, width)
    lower_rows = owned[:, :, : LINKS * block]
    inverse_rows = owned[:, :, LINKS * block :]
    inverse_all = lax.all_gather(inverse_rows, "row", axis=0, tiled=False)
    got = lax.all_to_all(payload, "row", 0, 0, tiled=False)
    got_updates = got[:, : LINKS * span].reshape(n_row, LINKS, span, cols)
    got_src = got[:, LINKS * span : LINKS * span + PAIR].reshape(STEPS, span, cols)
    got_lists = got[:, LINKS * span + PAIR, :LINKS]
    pending = []
    for k in range(STEPS):
        hit = (got_lists == k)[:, :, None, None]
        pending.append(got_src[k] - jnp.sum(jnp.where(hit, got_updates, 0.0), axis=(0, 1)))

    solved = jnp.zeros((STEPS, block, cols), jnp.float32)
    for k in range(STEPS):
        pieces = []
        for link_pos in range(LINKS):
            target = sep_links[k, link_pos]
            chosen = solved[jnp.maximum(target, 0)]
            pieces.append(jnp.where(target >= 0, chosen, 0.0).astype(jnp.bfloat16))
        stacked = jnp.concatenate(pieces, axis=0)
        residue = pending[k] - jnp.dot(
            lower_rows[k], stacked, preferred_element_type=jnp.float32
        )
        everyone = gather_row(residue.astype(jnp.bfloat16), n_row)
        full_residue = everyone.reshape(block, cols)
        inverse = inverse_all[:, k].reshape(block, block)
        result = jnp.dot(inverse, full_residue, preferred_element_type=jnp.float32)
        solved = solved.at[k].set(result)
    blocks_per = block // local_rows
    whole_field = solved.reshape(STEPS, n_row, n_src, PAIR, cols)
    own_rows = lax.dynamic_slice(
        whole_field,
        (my_row // blocks_per, 0, my_row % blocks_per, 0, 0),
        (1, n_row, 1, PAIR, cols),
    ).reshape(local_rows, cols)
    return (sub_field, own_rows)


def solution(mesh):
    return jax.shard_map(
        solve,
        mesh=mesh,
        in_specs=(
            P("row", "src"),
            P("row", None),
            P("row", None, None, None),
            P("row", None),
            P("row", "src"),
            P(("row", "src"), None),
            P(("row", "src"), None),
            P(),
            P(),
        ),
        out_specs=(P("row", "src"), P("row", "src")),
        check_vma=False,
    )
```

```python
import jax
import jax.numpy as jnp
from jax import lax
from jax.sharding import PartitionSpec as P

STEPS = 4
LINKS = 2
PAIR = 2


def gather_row(x, n_row):
    spread = jnp.broadcast_to(x[None], (n_row,) + x.shape)
    return lax.all_to_all(spread, "row", 0, 0, tiled=False)


def per_device(
    sub_source,
    sub_inverse,
    coupling,
    update_lists,
    sep_source,
    sep_inverse,
    sep_lower,
    factor_owner_slots,
    sep_links,
):
    n_row = lax.psum(1, "row")
    n_src = lax.psum(1, "src")
    cols = sub_source.shape[1]
    local_rows = sep_source.shape[0]
    block = sep_inverse.shape[1]
    span = PAIR * n_src
    my_row = lax.axis_index("row")

    factors = jnp.concatenate([sep_lower, sep_inverse], axis=1)
    width = factors.shape[1]
    slot_rows = lax.all_to_all(factors.reshape(n_row, PAIR, width), "row", 0, 0, tiled=False)
    owned = slot_rows[factor_owner_slots]
    owned = owned.reshape(STEPS, PAIR, width // block, n_src, n_row, PAIR)
    owned = owned.transpose(0, 1, 2, 4, 3, 5).reshape(STEPS, PAIR, width)
    owned = lax.all_gather(owned, "src", axis=0, tiled=False)
    owned, sub_source = lax.optimization_barrier((owned, sub_source))
    owned = owned.transpose(1, 0, 2, 3).reshape(STEPS, span, width)
    lower_rows = owned[:, :, : LINKS * block]
    inverse_rows = owned[:, :, LINKS * block :]
    inverse_all = lax.all_gather(inverse_rows, "row", axis=0, tiled=False)

    sub_field = jnp.dot(
        sub_inverse, sub_source.astype(jnp.bfloat16), preferred_element_type=jnp.float32
    )
    rounded = sub_field.astype(jnp.bfloat16)
    updates = jnp.einsum(
        "lmf,ft->lmt", coupling[0], rounded, preferred_element_type=jnp.float32
    )
    per_dest = updates.astype(jnp.bfloat16).reshape(LINKS, n_src, n_row, PAIR, cols)
    per_dest = per_dest.transpose(2, 0, 1, 3, 4).reshape(n_row, LINKS * span, cols)
    src_rows = sep_source.astype(jnp.bfloat16).reshape(n_row, PAIR, cols)
    lists = jnp.zeros((cols,), jnp.bfloat16).at[:LINKS].set(update_lists[0].astype(jnp.bfloat16))
    lists = jnp.broadcast_to(lists[None, None], (n_row, 1, cols))
    payload = jnp.concatenate([per_dest, src_rows, lists], axis=1)
    got = lax.all_to_all(payload, "row", 0, 0, tiled=False).astype(jnp.float32)
    got_updates = got[:, : LINKS * span].reshape(n_row, LINKS, span, cols)
    got_src = got[:, LINKS * span : LINKS * span + PAIR].reshape(STEPS, span, cols)
    got_lists = got[:, LINKS * span + PAIR, :LINKS]
    pending = []
    for k in range(STEPS):
        hit = (got_lists == k)[:, :, None, None]
        pending.append(got_src[k] - jnp.sum(jnp.where(hit, got_updates, 0.0), axis=(0, 1)))

    fields, rounded_fields = [], []
    for k in range(STEPS):
        residue = pending[k]
        if k >= 2:
            target = sep_links[k, 1]
            far = jnp.zeros((block, cols), jnp.bfloat16)
            for c in range(k - 1):
                far = jnp.where(target == c, rounded_fields[c], far)
            residue = residue - jnp.dot(
                lower_rows[k][:, block:], far, preferred_element_type=jnp.float32
            )
        if k >= 1:
            residue = residue - jnp.dot(
                lower_rows[k][:, :block], rounded_fields[k - 1], preferred_element_type=jnp.float32
            )
        everyone = gather_row(residue.astype(jnp.bfloat16), n_row)
        full_residue = everyone.reshape(block, cols)
        inverse = inverse_all[:, k].reshape(block, block)
        result = jnp.dot(inverse, full_residue, preferred_element_type=jnp.float32)
        fields.append(result)
        rounded_fields.append(result.astype(jnp.bfloat16))
    solved = jnp.stack(fields, axis=0)
    blocks_per = block // local_rows
    whole_field = solved.reshape(STEPS, n_row, n_src, PAIR, cols)
    own_rows = lax.dynamic_slice(
        whole_field,
        (my_row // blocks_per, 0, my_row % blocks_per, 0, 0),
        (1, n_row, 1, PAIR, cols),
    ).reshape(local_rows, cols)
    return (sub_field, own_rows)


def solution(mesh):
    return jax.shard_map(
        per_device,
        mesh=mesh,
        in_specs=(
            P("row", "src"),
            P("row", None),
            P("row", None, None, None),
            P("row", None),
            P("row", "src"),
            P(("row", "src"), None),
            P(("row", "src"), None),
            P(),
            P(),
        ),
        out_specs=(P("row", "src"), P("row", "src")),
        check_vma=False,
    )
```

```python
import jax
import jax.numpy as jnp
from jax import lax
from jax.sharding import PartitionSpec as P

STEPS = 4
LINKS = 2
PAIR = 2


def gather_row(x, n_row):
    spread = jnp.broadcast_to(x[None], (n_row,) + x.shape)
    return lax.all_to_all(spread, "row", 0, 0, tiled=False)


def per_device(
    sub_source,
    sub_inverse,
    coupling,
    update_lists,
    sep_source,
    sep_inverse,
    sep_lower,
    factor_owner_slots,
    sep_links,
):
    n_row = lax.psum(1, "row")
    n_src = lax.psum(1, "src")
    cols = sub_source.shape[1]
    local_rows = sep_source.shape[0]
    block = sep_inverse.shape[1]
    span = PAIR * n_src
    my_row = lax.axis_index("row")

    factors = jnp.concatenate([sep_lower, sep_inverse], axis=1)
    width = factors.shape[1]
    slot_rows = lax.all_to_all(factors.reshape(n_row, PAIR, width), "row", 0, 0, tiled=False)
    owned = slot_rows[factor_owner_slots]
    owned = owned.reshape(STEPS, PAIR, width // block, n_src, n_row, PAIR)
    owned = owned.transpose(0, 1, 2, 4, 3, 5).reshape(STEPS, PAIR, width)
    owned = lax.all_gather(owned, "src", axis=0, tiled=False)
    owned = owned.transpose(1, 0, 2, 3).reshape(STEPS, span, width)
    lower_rows = owned[:, :, : LINKS * block]
    inverse_rows = owned[:, :, LINKS * block :]
    inverse_all = lax.all_gather(inverse_rows, "row", axis=0, tiled=False)

    sub_field = jnp.dot(
        sub_inverse, sub_source.astype(jnp.bfloat16), preferred_element_type=jnp.float32
    )
    rounded = sub_field.astype(jnp.bfloat16)
    updates = jnp.einsum(
        "lmf,ft->lmt", coupling[0], rounded, preferred_element_type=jnp.float32
    )
    per_dest = updates.reshape(LINKS, n_src, n_row, PAIR, cols).transpose(2, 0, 1, 3, 4)
    per_dest = per_dest.reshape(n_row, LINKS * span, cols)
    src_rows = sep_source.reshape(n_row, PAIR, cols)
    lists = jnp.zeros((cols,), jnp.float32).at[:LINKS].set(update_lists[0].astype(jnp.float32))
    lists = jnp.broadcast_to(lists[None, None], (n_row, 1, cols))
    payload = jnp.concatenate([per_dest, src_rows, lists], axis=1)
    got = lax.all_to_all(payload, "row", 0, 0, tiled=False)
    got_updates = got[:, : LINKS * span].reshape(n_row, LINKS, span, cols)
    got_src = got[:, LINKS * span : LINKS * span + PAIR].reshape(STEPS, span, cols)
    got_lists = got[:, LINKS * span + PAIR, :LINKS]
    pending = []
    for k in range(STEPS):
        hit = (got_lists == k)[:, :, None, None]
        pending.append(got_src[k] - jnp.sum(jnp.where(hit, got_updates, 0.0), axis=(0, 1)))

    fields, rounded_fields = [], []
    for k in range(STEPS):
        residue = pending[k]
        if k >= 2:
            target = sep_links[k, 1]
            far = jnp.zeros((block, cols), jnp.bfloat16)
            for c in range(k - 1):
                far = jnp.where(target == c, rounded_fields[c], far)
            residue = residue - jnp.dot(
                lower_rows[k][:, block:], far, preferred_element_type=jnp.float32
            )
        if k >= 1:
            residue = residue - jnp.dot(
                lower_rows[k][:, :block], rounded_fields[k - 1], preferred_element_type=jnp.float32
            )
        everyone = gather_row(residue.astype(jnp.bfloat16), n_row)
        full_residue = everyone.reshape(block, cols)
        inverse = inverse_all[:, k].reshape(block, block)
        result = jnp.dot(inverse, full_residue, preferred_element_type=jnp.float32)
        fields.append(result)
        rounded_fields.append(result.astype(jnp.bfloat16))
    solved = jnp.stack(fields, axis=0)
    blocks_per = block // local_rows
    whole_field = solved.reshape(STEPS, n_row, n_src, PAIR, cols)
    own_rows = lax.dynamic_slice(
        whole_field,
        (my_row // blocks_per, 0, my_row % blocks_per, 0, 0),
        (1, n_row, 1, PAIR, cols),
    ).reshape(local_rows, cols)
    return (sub_field, own_rows)


def solution(mesh):
    return jax.shard_map(
        per_device,
        mesh=mesh,
        in_specs=(
            P("row", "src"),
            P("row", None),
            P("row", None, None, None),
            P("row", None),
            P("row", "src"),
            P(("row", "src"), None),
            P(("row", "src"), None),
            P(),
            P(),
        ),
        out_specs=(P("row", "src"), P("row", "src")),
        check_vma=False,
    )
```

```python
import jax
import jax.numpy as jnp
from jax import lax
from jax.sharding import PartitionSpec as P

STEPS = 4
LINKS = 2
PAIR = 2


def gather_row(x, n_row):
    spread = jnp.broadcast_to(x[None], (n_row,) + x.shape)
    return lax.all_to_all(spread, "row", 0, 0, tiled=False)


def per_device(
    sub_source,
    sub_inverse,
    coupling,
    update_lists,
    sep_source,
    sep_inverse,
    sep_lower,
    factor_owner_slots,
    sep_links,
):
    n_row = lax.psum(1, "row")
    n_src = lax.psum(1, "src")
    cols = sub_source.shape[1]
    local_rows = sep_source.shape[0]
    block = sep_inverse.shape[1]
    span = PAIR * n_src
    my_row = lax.axis_index("row")

    factors = jnp.concatenate([sep_lower, sep_inverse], axis=1)
    width = factors.shape[1]
    slot_rows = lax.all_to_all(factors.reshape(n_row, PAIR, width), "row", 0, 0, tiled=False)
    owned = slot_rows[factor_owner_slots]
    owned = owned.reshape(STEPS, PAIR, width // block, n_src, n_row, PAIR)
    owned = owned.transpose(0, 1, 2, 4, 3, 5).reshape(STEPS, PAIR, width)
    owned = lax.all_gather(owned, "src", axis=0, tiled=False)
    owned = owned.transpose(1, 0, 2, 3).reshape(STEPS, span, width)
    lower_rows = owned[:, :, : LINKS * block]
    inverse_rows = owned[:, :, LINKS * block :]
    inverse_all = lax.all_gather(inverse_rows, "row", axis=0, tiled=False)

    sub_field = jnp.dot(
        sub_inverse, sub_source.astype(jnp.bfloat16), preferred_element_type=jnp.float32
    )
    rounded = sub_field.astype(jnp.bfloat16)
    updates = jnp.einsum(
        "lmf,ft->lmt", coupling[0], rounded, preferred_element_type=jnp.float32
    )
    per_dest = updates.reshape(LINKS, n_src, n_row, PAIR, cols).transpose(2, 0, 1, 3, 4)
    per_dest = per_dest.reshape(n_row, LINKS * span, cols)
    src_rows = sep_source.reshape(n_row, PAIR, cols)
    lists = jnp.zeros((cols,), jnp.float32).at[:LINKS].set(update_lists[0].astype(jnp.float32))
    lists = jnp.broadcast_to(lists[None, None], (n_row, 1, cols))
    payload = jnp.concatenate([per_dest, src_rows, lists], axis=1)
    got = lax.all_to_all(payload, "row", 0, 0, tiled=False)
    got_updates = got[:, : LINKS * span].reshape(n_row, LINKS, span, cols)
    got_src = got[:, LINKS * span : LINKS * span + PAIR].reshape(STEPS, span, cols)
    got_lists = got[:, LINKS * span + PAIR, :LINKS]
    pending = []
    for k in range(STEPS):
        hit = (got_lists == k)[:, :, None, None]
        pending.append(got_src[k] - jnp.sum(jnp.where(hit, got_updates, 0.0), axis=(0, 1)))

    fields, rounded_fields = [], []
    for k in range(STEPS):
        residue = pending[k]
        if k >= 2:
            target = sep_links[k, 1]
            far = jnp.zeros((block, cols), jnp.bfloat16)
            for c in range(k - 1):
                far = jnp.where(target == c, rounded_fields[c], far)
            residue = residue - jnp.dot(
                lower_rows[k][:, block:], far, preferred_element_type=jnp.float32
            )
        if k >= 1:
            residue = residue - jnp.dot(
                lower_rows[k][:, :block], rounded_fields[k - 1], preferred_element_type=jnp.float32
            )
        everyone = gather_row(residue.astype(jnp.bfloat16), n_row)
        full_residue = everyone.reshape(block, cols)
        inverse = inverse_all[:, k].reshape(block, block)
        result = jnp.dot(inverse, full_residue, preferred_element_type=jnp.float32)
        fields.append(result)
        rounded_fields.append(result.astype(jnp.bfloat16))
    blocks_per = block // local_rows
    my_block = my_row // blocks_per
    my_part = my_row % blocks_per
    own_rows = jnp.zeros((local_rows, cols), jnp.float32)
    for k in range(STEPS):
        part = lax.dynamic_slice(
            fields[k].reshape(n_row, n_src, PAIR, cols),
            (0, my_part, 0, 0),
            (n_row, 1, PAIR, cols),
        ).reshape(local_rows, cols)
        own_rows = jnp.where(my_block == k, part, own_rows)
    return (sub_field, own_rows)


def solution(mesh):
    return jax.shard_map(
        per_device,
        mesh=mesh,
        in_specs=(
            P("row", "src"),
            P("row", None),
            P("row", None, None, None),
            P("row", None),
            P("row", "src"),
            P(("row", "src"), None),
            P(("row", "src"), None),
            P(),
            P(),
        ),
        out_specs=(P("row", "src"), P("row", "src")),
        check_vma=False,
    )
```

```python
import jax
import jax.numpy as jnp
from jax import lax
from jax.sharding import PartitionSpec as P

STEPS = 4
LINKS = 2
PAIR = 2


def gather_row(x, n_row):
    spread = jnp.broadcast_to(x[None], (n_row,) + x.shape)
    return lax.all_to_all(spread, "row", 0, 0, tiled=False)


def per_device(
    sub_source,
    sub_inverse,
    coupling,
    update_lists,
    sep_source,
    sep_inverse,
    sep_lower,
    factor_owner_slots,
    sep_links,
):
    n_row = lax.psum(1, "row")
    n_src = lax.psum(1, "src")
    cols = sub_source.shape[1]
    local_rows = sep_source.shape[0]
    block = sep_inverse.shape[1]
    span = PAIR * n_src
    my_row = lax.axis_index("row")

    factors = jnp.concatenate([sep_lower, sep_inverse], axis=1)
    width = factors.shape[1]
    slot_rows = lax.all_to_all(factors.reshape(n_row, PAIR, width), "row", 0, 0, tiled=False)
    owned = slot_rows[factor_owner_slots]
    owned = owned.reshape(STEPS, PAIR, width // block, n_src, n_row, PAIR)
    owned = owned.transpose(0, 1, 2, 4, 3, 5).reshape(STEPS, PAIR, width)
    owned = lax.all_gather(owned, "src", axis=0, tiled=False)
    owned = owned.transpose(1, 0, 2, 3).reshape(STEPS, span, width)
    lower_rows = owned[:, :, : LINKS * block]
    inverse_rows = owned[:, :, LINKS * block :]
    inverse_all = lax.all_gather(inverse_rows, "row", axis=0, tiled=False)

    sub_field = jnp.dot(
        sub_inverse, sub_source.astype(jnp.bfloat16), preferred_element_type=jnp.float32
    )
    rounded = sub_field.astype(jnp.bfloat16)
    sub_rows = coupling.shape[-1]
    grouped = coupling[0].reshape(LINKS, n_src, n_row, PAIR, sub_rows).transpose(2, 0, 1, 3, 4)
    grouped = grouped.reshape(n_row * LINKS * span, sub_rows)
    per_dest = jnp.dot(grouped, rounded, preferred_element_type=jnp.float32)
    per_dest = per_dest.reshape(n_row, LINKS * span, cols)
    src_rows = sep_source.reshape(n_row, PAIR, cols)
    lists = jnp.zeros((cols,), jnp.float32).at[:LINKS].set(update_lists[0].astype(jnp.float32))
    lists = jnp.broadcast_to(lists[None, None], (n_row, 1, cols))
    payload = jnp.concatenate([per_dest, src_rows, lists], axis=1)
    got = lax.all_to_all(payload, "row", 0, 0, tiled=False)
    got_updates = got[:, : LINKS * span].reshape(n_row, LINKS, span, cols)
    got_src = got[:, LINKS * span : LINKS * span + PAIR].reshape(STEPS, span, cols)
    got_lists = got[:, LINKS * span + PAIR, :LINKS]
    pending = []
    for k in range(STEPS):
        hit = (got_lists == k)[:, :, None, None]
        pending.append(got_src[k] - jnp.sum(jnp.where(hit, got_updates, 0.0), axis=(0, 1)))

    fields, rounded_fields = [], []
    for k in range(STEPS):
        residue = pending[k]
        if k >= 2:
            target = sep_links[k, 1]
            far = jnp.zeros((block, cols), jnp.bfloat16)
            for c in range(k - 1):
                far = jnp.where(target == c, rounded_fields[c], far)
            residue = residue - jnp.dot(
                lower_rows[k][:, block:], far, preferred_element_type=jnp.float32
            )
        if k >= 1:
            residue = residue - jnp.dot(
                lower_rows[k][:, :block], rounded_fields[k - 1], preferred_element_type=jnp.float32
            )
        everyone = gather_row(residue.astype(jnp.bfloat16), n_row)
        full_residue = everyone.reshape(block, cols)
        inverse = inverse_all[:, k].reshape(block, block)
        result = jnp.dot(inverse, full_residue, preferred_element_type=jnp.float32)
        fields.append(result)
        rounded_fields.append(result.astype(jnp.bfloat16))
    blocks_per = block // local_rows
    my_block = my_row // blocks_per
    my_part = my_row % blocks_per
    own_rows = jnp.zeros((local_rows, cols), jnp.float32)
    for k in range(STEPS):
        part = lax.dynamic_slice(
            fields[k].reshape(n_row, n_src, PAIR, cols),
            (0, my_part, 0, 0),
            (n_row, 1, PAIR, cols),
        ).reshape(local_rows, cols)
        own_rows = jnp.where(my_block == k, part, own_rows)
    return (sub_field, own_rows)


def solution(mesh):
    return jax.shard_map(
        per_device,
        mesh=mesh,
        in_specs=(
            P("row", "src"),
            P("row", None),
            P("row", None, None, None),
            P("row", None),
            P("row", "src"),
            P(("row", "src"), None),
            P(("row", "src"), None),
            P(),
            P(),
        ),
        out_specs=(P("row", "src"), P("row", "src")),
        check_vma=False,
    )
```

```python
import jax
import jax.numpy as jnp
from jax import lax
from jax.sharding import PartitionSpec as P

STEPS = 4
LINKS = 2
PAIR = 2


def gather_row(x, n_row):
    spread = jnp.broadcast_to(x[None], (n_row,) + x.shape)
    return lax.all_to_all(spread, "row", 0, 0, tiled=False)


def per_device(
    sub_source,
    sub_inverse,
    coupling,
    update_lists,
    sep_source,
    sep_inverse,
    sep_lower,
    factor_owner_slots,
    sep_links,
):
    n_row = lax.psum(1, "row")
    n_src = lax.psum(1, "src")
    cols = sub_source.shape[1]
    local_rows = sep_source.shape[0]
    block = sep_inverse.shape[1]
    span = PAIR * n_src
    my_row = lax.axis_index("row")

    factors = jnp.concatenate([sep_lower, sep_inverse], axis=1)
    width = factors.shape[1]
    slot_rows = lax.all_to_all(factors.reshape(n_row, PAIR, width), "row", 0, 0, tiled=False)
    owned = slot_rows[factor_owner_slots]
    owned = owned.reshape(STEPS, PAIR, width // block, n_src, n_row, PAIR)
    owned = owned.transpose(0, 1, 2, 4, 3, 5).reshape(STEPS, PAIR, width)
    owned = lax.all_gather(owned, "src", axis=0, tiled=False)
    owned = owned.transpose(1, 0, 2, 3).reshape(STEPS, span, width)
    lower_rows = owned[:, :, : LINKS * block]
    inverse_rows = owned[:, :, LINKS * block :]
    inverse_all = lax.all_gather(inverse_rows, "row", axis=0, tiled=False)

    sub_field = jnp.dot(
        sub_inverse, sub_source.astype(jnp.bfloat16), preferred_element_type=jnp.float32
    )
    rounded = sub_field.astype(jnp.bfloat16)
    updates = jnp.einsum(
        "lmf,ft->lmt", coupling[0], rounded, preferred_element_type=jnp.float32
    )
    spread = updates.reshape(LINKS, n_src, n_row, PAIR, cols)
    got_updates = lax.all_to_all(spread, "row", 2, 2, tiled=True)
    got_updates = got_updates.transpose(2, 0, 1, 3, 4).reshape(n_row, LINKS, span, cols)
    src_rows = sep_source.reshape(n_row, PAIR, cols)
    lists = jnp.zeros((cols,), jnp.float32).at[:LINKS].set(update_lists[0].astype(jnp.float32))
    lists = jnp.broadcast_to(lists[None, None], (n_row, 1, cols))
    got = lax.all_to_all(jnp.concatenate([src_rows, lists], axis=1), "row", 0, 0, tiled=False)
    got_src = got[:, :PAIR].reshape(STEPS, span, cols)
    got_lists = got[:, PAIR, :LINKS]
    pending = []
    for k in range(STEPS):
        hit = (got_lists == k)[:, :, None, None]
        pending.append(got_src[k] - jnp.sum(jnp.where(hit, got_updates, 0.0), axis=(0, 1)))

    fields, rounded_fields = [], []
    for k in range(STEPS):
        residue = pending[k]
        if k >= 2:
            target = sep_links[k, 1]
            far = jnp.zeros((block, cols), jnp.bfloat16)
            for c in range(k - 1):
                far = jnp.where(target == c, rounded_fields[c], far)
            residue = residue - jnp.dot(
                lower_rows[k][:, block:], far, preferred_element_type=jnp.float32
            )
        if k >= 1:
            residue = residue - jnp.dot(
                lower_rows[k][:, :block], rounded_fields[k - 1], preferred_element_type=jnp.float32
            )
        everyone = gather_row(residue.astype(jnp.bfloat16), n_row)
        full_residue = everyone.reshape(block, cols)
        inverse = inverse_all[:, k].reshape(block, block)
        result = jnp.dot(inverse, full_residue, preferred_element_type=jnp.float32)
        fields.append(result)
        rounded_fields.append(result.astype(jnp.bfloat16))
    blocks_per = block // local_rows
    my_block = my_row // blocks_per
    my_part = my_row % blocks_per
    own_rows = jnp.zeros((local_rows, cols), jnp.float32)
    for k in range(STEPS):
        part = lax.dynamic_slice(
            fields[k].reshape(n_row, n_src, PAIR, cols),
            (0, my_part, 0, 0),
            (n_row, 1, PAIR, cols),
        ).reshape(local_rows, cols)
        own_rows = jnp.where(my_block == k, part, own_rows)
    return (sub_field, own_rows)


def solution(mesh):
    return jax.shard_map(
        per_device,
        mesh=mesh,
        in_specs=(
            P("row", "src"),
            P("row", None),
            P("row", None, None, None),
            P("row", None),
            P("row", "src"),
            P(("row", "src"), None),
            P(("row", "src"), None),
            P(),
            P(),
        ),
        out_specs=(P("row", "src"), P("row", "src")),
        check_vma=False,
    )
```

```python
import jax
import jax.numpy as jnp
from jax import lax
from jax.sharding import PartitionSpec as P

STEPS = 4
LINKS = 2
PAIR = 2


def gather_row(x, n_row):
    spread = jnp.broadcast_to(x[None], (n_row,) + x.shape)
    return lax.all_to_all(spread, "row", 0, 0, tiled=False)


def per_device(
    sub_source,
    sub_inverse,
    coupling,
    update_lists,
    sep_source,
    sep_inverse,
    sep_lower,
    factor_owner_slots,
    sep_links,
):
    n_row = lax.psum(1, "row")
    n_src = lax.psum(1, "src")
    cols = sub_source.shape[1]
    local_rows = sep_source.shape[0]
    block = sep_inverse.shape[1]
    span = PAIR * n_src
    my_row = lax.axis_index("row")

    factors = jnp.concatenate([sep_lower, sep_inverse], axis=1)
    width = factors.shape[1]
    slot_rows = lax.all_to_all(factors.reshape(n_row, PAIR, width), "row", 0, 0, tiled=False)
    owned = slot_rows[factor_owner_slots]
    owned = owned.reshape(STEPS, PAIR, width // block, n_src, n_row, PAIR)
    owned = owned.transpose(0, 1, 2, 4, 3, 5).reshape(STEPS, PAIR, width)
    owned = lax.all_gather(owned, "src", axis=0, tiled=False)
    owned = owned.transpose(1, 0, 2, 3).reshape(STEPS, span, width)
    lower_rows = owned[:, :, : LINKS * block]
    inverse_rows = owned[:, :, LINKS * block :]
    inverse_all = lax.all_gather(inverse_rows, "row", axis=0, tiled=False)

    sub_field = jnp.dot(
        sub_inverse, sub_source.astype(jnp.bfloat16), preferred_element_type=jnp.float32
    )
    rounded = sub_field.astype(jnp.bfloat16)
    updates = jnp.einsum(
        "lmf,ft->lmt", coupling[0], rounded, preferred_element_type=jnp.float32
    )
    blocks_per = block // local_rows
    my_shard = my_row % blocks_per
    extra = jnp.zeros((n_src, n_row, PAIR, cols), jnp.float32)
    extra = lax.dynamic_update_slice(
        extra, sep_source.reshape(1, n_row, PAIR, cols), (my_shard, 0, 0, 0)
    )
    lists = jnp.zeros((cols,), jnp.float32).at[:LINKS].set(update_lists[0].astype(jnp.float32))
    lists = jnp.broadcast_to(lists[None, None, None], (1, n_row, PAIR, cols))
    extra = lax.dynamic_update_slice(extra, lists, ((my_shard + n_src // 2) % n_src, 0, 0, 0))
    spread = jnp.concatenate(
        [updates.reshape(LINKS, n_src, n_row, PAIR, cols), extra[None]], axis=0
    )
    got = lax.all_to_all(spread, "row", 2, 2, tiled=True)
    got_updates = got[:LINKS].transpose(2, 0, 1, 3, 4).reshape(n_row, LINKS, span, cols)
    got_src = jnp.stack(
        [
            jnp.stack([got[LINKS, q, k * blocks_per + q] for q in range(n_src)]).reshape(span, cols)
            for k in range(STEPS)
        ]
    )
    got_lists = jnp.stack(
        [got[LINKS, (i % blocks_per + n_src // 2) % n_src, i, 0, :LINKS] for i in range(n_row)]
    )
    pending = []
    for k in range(STEPS):
        hit = (got_lists == k)[:, :, None, None]
        pending.append(got_src[k] - jnp.sum(jnp.where(hit, got_updates, 0.0), axis=(0, 1)))

    fields, rounded_fields = [], []
    for k in range(STEPS):
        residue = pending[k]
        if k >= 2:
            target = sep_links[k, 1]
            far = jnp.zeros((block, cols), jnp.bfloat16)
            for c in range(k - 1):
                far = jnp.where(target == c, rounded_fields[c], far)
            residue = residue - jnp.dot(
                lower_rows[k][:, block:], far, preferred_element_type=jnp.float32
            )
        if k >= 1:
            residue = residue - jnp.dot(
                lower_rows[k][:, :block], rounded_fields[k - 1], preferred_element_type=jnp.float32
            )
        everyone = gather_row(residue.astype(jnp.bfloat16), n_row)
        full_residue = everyone.reshape(block, cols)
        inverse = inverse_all[:, k].reshape(block, block)
        result = jnp.dot(inverse, full_residue, preferred_element_type=jnp.float32)
        fields.append(result)
        rounded_fields.append(result.astype(jnp.bfloat16))
    my_block = my_row // blocks_per
    my_part = my_row % blocks_per
    own_rows = jnp.zeros((local_rows, cols), jnp.float32)
    for k in range(STEPS):
        part = lax.dynamic_slice(
            fields[k].reshape(n_row, n_src, PAIR, cols),
            (0, my_part, 0, 0),
            (n_row, 1, PAIR, cols),
        ).reshape(local_rows, cols)
        own_rows = jnp.where(my_block == k, part, own_rows)
    return (sub_field, own_rows)


def solution(mesh):
    return jax.shard_map(
        per_device,
        mesh=mesh,
        in_specs=(
            P("row", "src"),
            P("row", None),
            P("row", None, None, None),
            P("row", None),
            P("row", "src"),
            P(("row", "src"), None),
            P(("row", "src"), None),
            P(),
            P(),
        ),
        out_specs=(P("row", "src"), P("row", "src")),
        check_vma=False,
    )
```

```python
import jax
import jax.numpy as jnp
from jax import lax
from jax.sharding import PartitionSpec as P

STEPS = 4
LINKS = 2
PAIR = 2


def gather_row(x, n_row):
    spread = jnp.broadcast_to(x[None], (n_row,) + x.shape)
    return lax.all_to_all(spread, "row", 0, 0, tiled=False)


def per_device(
    sub_source,
    sub_inverse,
    coupling,
    update_lists,
    sep_source,
    sep_inverse,
    sep_lower,
    factor_owner_slots,
    sep_links,
):
    n_row = lax.psum(1, "row")
    n_src = lax.psum(1, "src")
    cols = sub_source.shape[1]
    local_rows = sep_source.shape[0]
    block = sep_inverse.shape[1]
    span = PAIR * n_src
    my_row = lax.axis_index("row")

    factors = jnp.concatenate([sep_lower, sep_inverse], axis=1)
    width = factors.shape[1]
    my_list = jnp.zeros((width,), jnp.bfloat16).at[:LINKS].set(update_lists[0].astype(jnp.bfloat16))
    my_list = jnp.broadcast_to(my_list[None, None], (n_row, 1, width))
    sent = jnp.concatenate([factors.reshape(n_row, PAIR, width), my_list], axis=1)
    slot_rows = lax.all_to_all(sent, "row", 0, 0, tiled=False)
    got_lists = slot_rows[:, PAIR, :LINKS].astype(jnp.float32)
    owned = slot_rows[:, :PAIR][factor_owner_slots]
    owned = owned.reshape(STEPS, PAIR, width // block, n_src, n_row, PAIR)
    owned = owned.transpose(0, 1, 2, 4, 3, 5).reshape(STEPS, PAIR, width)
    owned = lax.all_gather(owned, "src", axis=0, tiled=False)
    owned = owned.transpose(1, 0, 2, 3).reshape(STEPS, span, width)
    lower_rows = owned[:, :, : LINKS * block]
    inverse_rows = owned[:, :, LINKS * block :]
    inverse_all = lax.all_gather(inverse_rows, "row", axis=0, tiled=False)

    sub_field = jnp.dot(
        sub_inverse, sub_source.astype(jnp.bfloat16), preferred_element_type=jnp.float32
    )
    rounded = sub_field.astype(jnp.bfloat16)
    updates = jnp.einsum(
        "lmf,ft->lmt", coupling[0], rounded, preferred_element_type=jnp.float32
    )
    per_dest = updates.reshape(LINKS, n_src, n_row, PAIR, cols).transpose(2, 0, 1, 3, 4)
    per_dest = per_dest.reshape(n_row, LINKS * span, cols)
    src_rows = sep_source.reshape(n_row, PAIR, cols)
    payload = jnp.concatenate([per_dest, src_rows], axis=1)
    got = lax.all_to_all(payload, "row", 0, 0, tiled=False)
    got_updates = got[:, : LINKS * span].reshape(n_row, LINKS, span, cols)
    got_src = got[:, LINKS * span : LINKS * span + PAIR].reshape(STEPS, span, cols)
    pending = []
    for k in range(STEPS):
        hit = (got_lists == k)[:, :, None, None]
        pending.append(got_src[k] - jnp.sum(jnp.where(hit, got_updates, 0.0), axis=(0, 1)))

    fields, rounded_fields = [], []
    for k in range(STEPS):
        residue = pending[k]
        if k >= 2:
            target = sep_links[k, 1]
            far = jnp.zeros((block, cols), jnp.bfloat16)
            for c in range(k - 1):
                far = jnp.where(target == c, rounded_fields[c], far)
            residue = residue - jnp.dot(
                lower_rows[k][:, block:], far, preferred_element_type=jnp.float32
            )
        if k >= 1:
            residue = residue - jnp.dot(
                lower_rows[k][:, :block], rounded_fields[k - 1], preferred_element_type=jnp.float32
            )
        everyone = gather_row(residue.astype(jnp.bfloat16), n_row)
        full_residue = everyone.reshape(block, cols)
        inverse = inverse_all[:, k].reshape(block, block)
        result = jnp.dot(inverse, full_residue, preferred_element_type=jnp.float32)
        fields.append(result)
        rounded_fields.append(result.astype(jnp.bfloat16))
    blocks_per = block // local_rows
    my_block = my_row // blocks_per
    my_part = my_row % blocks_per
    own_rows = jnp.zeros((local_rows, cols), jnp.float32)
    for k in range(STEPS):
        part = lax.dynamic_slice(
            fields[k].reshape(n_row, n_src, PAIR, cols),
            (0, my_part, 0, 0),
            (n_row, 1, PAIR, cols),
        ).reshape(local_rows, cols)
        own_rows = jnp.where(my_block == k, part, own_rows)
    return (sub_field, own_rows)


def solution(mesh):
    return jax.shard_map(
        per_device,
        mesh=mesh,
        in_specs=(
            P("row", "src"),
            P("row", None),
            P("row", None, None, None),
            P("row", None),
            P("row", "src"),
            P(("row", "src"), None),
            P(("row", "src"), None),
            P(),
            P(),
        ),
        out_specs=(P("row", "src"), P("row", "src")),
        check_vma=False,
    )
```

```python
import jax
import jax.numpy as jnp
from jax import lax
from jax.sharding import PartitionSpec as P

STEPS = 4
LINKS = 2
PAIR = 2


def gather_row(x, n_row):
    spread = jnp.broadcast_to(x[None], (n_row,) + x.shape)
    return lax.all_to_all(spread, "row", 0, 0, tiled=False)


def per_device(
    sub_source,
    sub_inverse,
    coupling,
    update_lists,
    sep_source,
    sep_inverse,
    sep_lower,
    factor_owner_slots,
    sep_links,
):
    n_row = lax.psum(1, "row")
    n_src = lax.psum(1, "src")
    cols = sub_source.shape[1]
    local_rows = sep_source.shape[0]
    block = sep_inverse.shape[1]
    span = PAIR * n_src
    my_row = lax.axis_index("row")

    factors = jnp.concatenate([sep_lower, sep_inverse], axis=1)
    width = factors.shape[1]
    my_list = jnp.zeros((width,), jnp.bfloat16).at[:LINKS].set(update_lists[0].astype(jnp.bfloat16))
    my_list = jnp.broadcast_to(my_list[None, None], (n_row, 1, width))
    sent = jnp.concatenate([factors.reshape(n_row, PAIR, width), my_list], axis=1)
    slot_rows = lax.all_to_all(sent, "row", 0, 0, tiled=False)
    got_lists = slot_rows[:, PAIR, :LINKS].astype(jnp.float32)
    owned = slot_rows[:, :PAIR][factor_owner_slots]
    owned = owned.reshape(STEPS, PAIR, width // block, n_src, n_row, PAIR)
    owned = owned.transpose(0, 1, 2, 4, 3, 5).reshape(STEPS, PAIR, width)
    owned = lax.all_gather(owned, "src", axis=0, tiled=False)
    owned = owned.transpose(1, 0, 2, 3).reshape(STEPS, span, width)
    lower_rows = owned[:, :, : LINKS * block]
    inverse_rows = owned[:, :, LINKS * block :]
    inverse_all = lax.all_gather(inverse_rows, "row", axis=1, tiled=False)

    sub_field = jnp.dot(
        sub_inverse, sub_source.astype(jnp.bfloat16), preferred_element_type=jnp.float32
    )
    rounded = sub_field.astype(jnp.bfloat16)
    updates = jnp.einsum(
        "lmf,ft->lmt", coupling[0], rounded, preferred_element_type=jnp.float32
    )
    per_dest = updates.reshape(LINKS, n_src, n_row, PAIR, cols).transpose(2, 0, 1, 3, 4)
    per_dest = per_dest.reshape(n_row, LINKS * span, cols)
    src_rows = sep_source.reshape(n_row, PAIR, cols)
    payload = jnp.concatenate([per_dest, src_rows], axis=1)
    got = lax.all_to_all(payload, "row", 0, 0, tiled=False)
    got_updates = got[:, : LINKS * span].reshape(n_row, LINKS, span, cols)
    got_src = got[:, LINKS * span : LINKS * span + PAIR].reshape(STEPS, span, cols)
    pending = []
    for k in range(STEPS):
        hit = (got_lists == k)[:, :, None, None]
        pending.append(got_src[k] - jnp.sum(jnp.where(hit, got_updates, 0.0), axis=(0, 1)))

    fields, rounded_fields = [], []
    for k in range(STEPS):
        residue = pending[k]
        if k >= 2:
            target = sep_links[k, 1]
            far = jnp.zeros((block, cols), jnp.bfloat16)
            for c in range(k - 1):
                far = jnp.where(target == c, rounded_fields[c], far)
            residue = residue - jnp.dot(
                lower_rows[k][:, block:], far, preferred_element_type=jnp.float32
            )
        if k >= 1:
            residue = residue - jnp.dot(
                lower_rows[k][:, :block], rounded_fields[k - 1], preferred_element_type=jnp.float32
            )
        everyone = gather_row(residue.astype(jnp.bfloat16), n_row)
        full_residue = everyone.reshape(block, cols)
        inverse = inverse_all[k].reshape(block, block)
        result = jnp.dot(inverse, full_residue, preferred_element_type=jnp.float32)
        fields.append(result)
        rounded_fields.append(result.astype(jnp.bfloat16))
    blocks_per = block // local_rows
    my_block = my_row // blocks_per
    my_part = my_row % blocks_per
    own_rows = jnp.zeros((local_rows, cols), jnp.float32)
    for k in range(STEPS):
        part = lax.dynamic_slice(
            fields[k].reshape(n_row, n_src, PAIR, cols),
            (0, my_part, 0, 0),
            (n_row, 1, PAIR, cols),
        ).reshape(local_rows, cols)
        own_rows = jnp.where(my_block == k, part, own_rows)
    return (sub_field, own_rows)


def solution(mesh):
    return jax.shard_map(
        per_device,
        mesh=mesh,
        in_specs=(
            P("row", "src"),
            P("row", None),
            P("row", None, None, None),
            P("row", None),
            P("row", "src"),
            P(("row", "src"), None),
            P(("row", "src"), None),
            P(),
            P(),
        ),
        out_specs=(P("row", "src"), P("row", "src")),
        check_vma=False,
    )
```

```python
import jax
import jax.numpy as jnp
from jax import lax
from jax.sharding import PartitionSpec as P

STEPS = 4
LINKS = 2
PAIR = 2


def gather_row(x, n_row):
    spread = jnp.broadcast_to(x[None], (n_row,) + x.shape)
    return lax.all_to_all(spread, "row", 0, 0, tiled=False)


def per_device(
    sub_source,
    sub_inverse,
    coupling,
    update_lists,
    sep_source,
    sep_inverse,
    sep_lower,
    factor_owner_slots,
    sep_links,
):
    n_row = lax.psum(1, "row")
    n_src = lax.psum(1, "src")
    cols = sub_source.shape[1]
    local_rows = sep_source.shape[0]
    block = sep_inverse.shape[1]
    span = PAIR * n_src
    my_row = lax.axis_index("row")

    factors = jnp.concatenate([sep_lower, sep_inverse], axis=1)
    width = factors.shape[1]
    my_list = jnp.zeros((width,), jnp.bfloat16).at[:LINKS].set(update_lists[0].astype(jnp.bfloat16))
    my_list = jnp.broadcast_to(my_list[None, None], (n_row, 1, width))
    sent = jnp.concatenate([factors.reshape(n_row, PAIR, width), my_list], axis=1)
    slot_rows = lax.all_to_all(sent, "row", 0, 0, tiled=False)
    got_lists = slot_rows[:, PAIR, :LINKS].astype(jnp.float32)
    owned = slot_rows[:, :PAIR][factor_owner_slots]
    owned = owned.reshape(STEPS, PAIR, width // block, n_src, n_row, PAIR)
    owned = owned.transpose(0, 1, 2, 4, 3, 5).reshape(STEPS, PAIR, width)
    owned = lax.all_gather(owned, "src", axis=0, tiled=False)
    owned = owned.transpose(1, 0, 2, 3).reshape(STEPS, span, width)
    lower_rows = owned[:, :, : LINKS * block]
    inverse_rows = owned[:, :, LINKS * block :]
    inverse_all = lax.all_gather(inverse_rows, "row", axis=0, tiled=False)

    sub_field = jnp.dot(
        sub_inverse, sub_source.astype(jnp.bfloat16), preferred_element_type=jnp.float32
    )
    rounded = sub_field.astype(jnp.bfloat16)
    updates = jnp.einsum(
        "lmf,ft->lmt", coupling[0], rounded, preferred_element_type=jnp.float32
    )
    per_dest = updates.reshape(LINKS, n_src, n_row, PAIR, cols).transpose(2, 0, 1, 3, 4)
    per_dest = per_dest.reshape(n_row, LINKS * span, cols)
    src_rows = sep_source.reshape(n_row, PAIR, cols)
    payload = jnp.concatenate([per_dest, src_rows], axis=1)
    got = lax.all_to_all(payload, "row", 0, 0, tiled=False)
    got_updates = got[:, : LINKS * span].reshape(n_row, LINKS, span, cols)
    got_src = got[:, LINKS * span : LINKS * span + PAIR].reshape(STEPS, span, cols)
    hit = (got_lists[:, :, None] == jnp.arange(STEPS, dtype=jnp.float32)).astype(jnp.float32)
    summed = jnp.einsum(
        "ilk,ilpc->kpc", hit, got_updates, precision=lax.Precision.HIGHEST,
        preferred_element_type=jnp.float32,
    )
    pending = [got_src[k] - summed[k] for k in range(STEPS)]

    fields, rounded_fields = [], []
    for k in range(STEPS):
        residue = pending[k]
        if k >= 2:
            target = sep_links[k, 1]
            far = jnp.zeros((block, cols), jnp.bfloat16)
            for c in range(k - 1):
                far = jnp.where(target == c, rounded_fields[c], far)
            residue = residue - jnp.dot(
                lower_rows[k][:, block:], far, preferred_element_type=jnp.float32
            )
        if k >= 1:
            residue = residue - jnp.dot(
                lower_rows[k][:, :block], rounded_fields[k - 1], preferred_element_type=jnp.float32
            )
        everyone = gather_row(residue.astype(jnp.bfloat16), n_row)
        full_residue = everyone.reshape(block, cols)
        inverse = inverse_all[:, k].reshape(block, block)
        result = jnp.dot(inverse, full_residue, preferred_element_type=jnp.float32)
        fields.append(result)
        rounded_fields.append(result.astype(jnp.bfloat16))
    blocks_per = block // local_rows
    my_block = my_row // blocks_per
    my_part = my_row % blocks_per
    own_rows = jnp.zeros((local_rows, cols), jnp.float32)
    for k in range(STEPS):
        part = lax.dynamic_slice(
            fields[k].reshape(n_row, n_src, PAIR, cols),
            (0, my_part, 0, 0),
            (n_row, 1, PAIR, cols),
        ).reshape(local_rows, cols)
        own_rows = jnp.where(my_block == k, part, own_rows)
    return (sub_field, own_rows)


def solution(mesh):
    return jax.shard_map(
        per_device,
        mesh=mesh,
        in_specs=(
            P("row", "src"),
            P("row", None),
            P("row", None, None, None),
            P("row", None),
            P("row", "src"),
            P(("row", "src"), None),
            P(("row", "src"), None),
            P(),
            P(),
        ),
        out_specs=(P("row", "src"), P("row", "src")),
        check_vma=False,
    )
```
